32 devices in a mesh: grp: 4 (over y, core), dp: 8 (over z, x).
Axes of the slice: x: 2, y: 2, z: 4, core: 2. Of those that a mesh axis runs over, the one named last changes fastest.
Arguments:
- queries: bfloat16 [8, 4, 128, 2048], P('dp', 'grp'), may hold values from -18 to 18
- mem_keys: bfloat16 [8, 4, 256, 2048], P('dp', 'grp'), may hold values from -18 to 18
- mem_values: bfloat16 [8, 4, 256, 2048], P('dp', 'grp'), may hold values from -48 to 48
- lengths: int32 [8, 4], P('dp'), may hold values from 128 to 256, as said below
- mates: int32 [8, 4, 4], P('dp'), may hold values 0 or 1
- out_grad: bfloat16 [8, 4, 128, 2048], P('dp', 'grp'), may hold values from -6 to 6
- mlp_input: bfloat16 [8, 4, 128, 4096], P('dp', 'grp'), may hold values from -6 to 6
- gate_pre: bfloat16 [8, 4, 128, 5632], P('dp', 'grp'), may hold values from -6 to 6
- hidden_grad: bfloat16 [8, 4, 128, 5632], P('dp', 'grp'), may hold values from -0.09375 to 0.09375
Outputs:
- attn_out: bfloat16 [8, 4, 128, 2048], P('dp', 'grp')
- q_grad: bfloat16 [8, 4, 128, 2048], P('dp', 'grp')
- up_grad: float32 [4096, 5632], P(None, ('grp', 'dp'))
The draws below stay inside these ranges and needn't reach their ends.
Inputs may be any that keep to these rules, and one draw needn't show every extreme that they name: `lengths`: each is a multiple of 128; in every group some document has 256. `mates`: A document reads its own previous context whatever its diagonal entry.
All inputs are finite; a program needn't handle non-finite values. No bound on the sum of `mates` on one device may be relied on, other than what follows from the above.
Results may differ from the reference program's by a relative error of at most 0.025.
Values may be sent and summed in bfloat16 or wider, within the bound.
A program may use at most 128 MiB of HBM per device.

```python
import jax
import jax.numpy as jnp
from jax import lax

D = 4096
HEAD_DIM = 128
HEADS = 16
FF = 5632
BLOCK = 128
MAXMEM = 256
Q = 128
GROUPS = 8
MEMBERS = 4
TOKENS = 4096


def shared_draw(key):
    query_key = jax.random.fold_in(key, 101)
    memory_key = jax.random.fold_in(key, 202)
    query_shape = (GROUPS, MEMBERS, Q, HEADS, HEAD_DIM)
    memory_shape = (GROUPS, MEMBERS, MAXMEM, HEADS, HEAD_DIM)
    query_vals = 1.5 * jnp.clip(jax.random.normal(query_key, query_shape, jnp.float32), -6.0, 6.0)
    memory_vals = jnp.clip(jax.random.normal(memory_key, memory_shape, jnp.float32), -6.0, 6.0)
    query_flat = query_vals.reshape(GROUPS, MEMBERS, Q, HEADS * HEAD_DIM)
    memory_flat = memory_vals.reshape(GROUPS, MEMBERS, MAXMEM, HEADS * HEAD_DIM)
    return (query_flat, memory_flat)


def draw_queries(key, part):
    return shared_draw(key)[0].astype(jnp.bfloat16)


def draw_mem_keys(key, part):
    return shared_draw(key)[1].astype(jnp.bfloat16)


def draw_lengths(key, part):
    granules = jax.random.randint(jax.random.fold_in(key, 7), (GROUPS, MEMBERS), 1, MAXMEM // BLOCK + 1)
    longest = jax.random.randint(jax.random.fold_in(key, 8), (GROUPS, 1), 0, MEMBERS)
    granules = jnp.where(jnp.arange(MEMBERS)[None, :] == longest, MAXMEM // BLOCK, granules)
    return (granules * BLOCK).astype(jnp.int32)


def plant(entries, key, low, high):
    place = [jax.random.randint(jax.random.fold_in(key, axis), (), 0, length) for axis, length in enumerate(entries.shape)]
    main_axis = entries.shape.index(max(entries.shape))
    beside = place[:main_axis] + [(place[main_axis] + 1) % entries.shape[main_axis]] + place[main_axis + 1:]
    return entries.at[tuple(place)].set(low).at[tuple(beside)].set(high)


def steps_of(own_key, shape, cuts, least, largest):
    def one(dim, shards_of):
        draws = jax.random.uniform(jax.random.fold_in(jax.random.fold_in(own_key, 6), dim), (shards_of,), jnp.float32, least / len(cuts), largest / len(cuts))
        return jnp.repeat(jnp.exp(draws), shape[dim] // shards_of).reshape((-1,) + (1,) * (len(shape) - dim - 1))

    factor_of = one(*cuts[0])
    for cut in cuts[1:]:
        factor_of = factor_of * one(*cut)
    return factor_of


def normal_values(rng, extent, scale, limit, cuts=(), kind=jnp.bfloat16):
    loudness = steps_of(rng, extent, cuts, -0.22, 0.18) if cuts else 1.0
    values = jax.random.normal(rng, extent, jnp.float32) * scale * loudness
    return jnp.minimum(jnp.maximum(values, -limit), limit).astype(kind)


def setup_inputs(seed: int = 0) -> dict:
    seeds = jax.random.split(jax.random.key(seed), 10)
    queries = draw_queries(jax.random.fold_in(seeds[9], 71), 0)
    mem_keys = draw_mem_keys(jax.random.fold_in(seeds[9], 71), 0)
    mem_values = normal_values(seeds[2], (GROUPS, MEMBERS, MAXMEM, HEADS * HEAD_DIM), 8.0, 48.0, ((0, 8), (1, 4)))
    lengths = draw_lengths(jax.random.fold_in(seeds[9], 71), 0)
    mates = plant((jax.random.randint(seeds[4], (GROUPS, MEMBERS, MEMBERS), 0, 4) < 3).astype(jnp.int32), jax.random.fold_in(seeds[4], 1), 0, 1)
    out_grad = normal_values(seeds[5], (GROUPS, MEMBERS, Q, HEADS * HEAD_DIM), 1.0, 6.0, ((0, 8), (1, 4)))
    mlp_input = normal_values(seeds[6], (GROUPS, MEMBERS, Q, D), 1.0, 6.0, ((0, 8), (1, 4)))
    gate_pre = normal_values(seeds[7], (GROUPS, MEMBERS, Q, FF), 1.0, 6.0, ((0, 8), (1, 4)))
    hidden_grad = normal_values(seeds[8], (GROUPS, MEMBERS, Q, FF), TOKENS ** -0.5, 0.09375, ((0, 8), (1, 4)))
    return {"queries": queries, "mem_keys": mem_keys, "mem_values": mem_values, "lengths": lengths, "mates": mates, "out_grad": out_grad, "mlp_input": mlp_input, "gate_pre": gate_pre, "hidden_grad": hidden_grad}


def head_pass(query_head, key_head, value_head, grad_head, key_mask):
    inv_root = HEAD_DIM ** -0.5
    scores = jnp.dot(query_head, key_head.T, preferred_element_type=jnp.float32) * inv_root
    scores = jnp.where(key_mask, scores, -1e30)
    highest = jnp.max(scores, axis=1, keepdims=True)
    weights = jnp.exp(scores - highest)
    row_total = jnp.sum(weights, axis=1, keepdims=True)
    weights_bf = (weights / row_total).astype(jnp.bfloat16)
    result = jnp.dot(weights_bf, value_head, preferred_element_type=jnp.float32).astype(jnp.bfloat16)
    grad_weights = jnp.dot(grad_head, value_head.T, preferred_element_type=jnp.float32)
    row_dot = jnp.sum(grad_head.astype(jnp.float32) * result.astype(jnp.float32), axis=1, keepdims=True)
    grad_scores = (weights_bf.astype(jnp.float32) * (grad_weights - row_dot)).astype(jnp.bfloat16)
    grad_query = (jnp.dot(grad_scores, key_head, preferred_element_type=jnp.float32) * inv_root).astype(jnp.bfloat16)
    return result, grad_query


def split_heads(block, row_count):
    return block.reshape(MEMBERS * row_count, HEADS, HEAD_DIM).transpose(1, 0, 2)


def join_heads(block):
    return block.transpose(1, 0, 2).reshape(MEMBERS, Q, HEADS * HEAD_DIM)


def group_pass(inputs):
    query_grp, key_grp, value_grp, grad_grp, length_row, mates_row = inputs
    allowed = (mates_row > 0) | jnp.eye(MEMBERS, dtype=bool)
    live_keys = jnp.arange(MAXMEM, dtype=jnp.int32)[None, :] < length_row[:, None]
    key_mask = jnp.broadcast_to(allowed[:, None, :, None] & live_keys[None, None, :, :], (MEMBERS, Q, MEMBERS, MAXMEM))
    key_mask = key_mask.reshape(MEMBERS * Q, MEMBERS * MAXMEM)

    def one_head(pieces):
        return head_pass(pieces[0], pieces[1], pieces[2], pieces[3], key_mask)

    results, gradients = lax.map(one_head, (split_heads(query_grp, Q), split_heads(key_grp, MAXMEM), split_heads(value_grp, MAXMEM), split_heads(grad_grp, Q)))
    return join_heads(results), join_heads(gradients)


def reference(queries, mem_keys, mem_values, lengths, mates, out_grad, mlp_input, gate_pre, hidden_grad):
    attn_out, q_grad = lax.map(group_pass, (queries, mem_keys, mem_values, out_grad, lengths, mates))

    def add_group(running, triple):
        inputs_grp, cot_grp, gate_grp = triple
        up_cot = (cot_grp.astype(jnp.float32) * jax.nn.silu(gate_grp.astype(jnp.float32))).astype(jnp.bfloat16)
        slab = jnp.dot(inputs_grp.reshape(MEMBERS * Q, D).T, up_cot.reshape(MEMBERS * Q, FF), preferred_element_type=jnp.float32)
        rounded = lax.optimization_barrier(slab.astype(jnp.bfloat16))
        return running + rounded.astype(jnp.float32), None

    up_grad, _ = lax.scan(add_group, jnp.zeros((D, FF), jnp.float32), (mlp_input, hidden_grad, gate_pre))
    return attn_out, q_grad, up_grad
```

```python
import functools
import math

import jax
import jax.numpy as jnp
from jax import lax
from jax.experimental import pallas as pl
from jax.experimental.pallas import tpu as pltpu
from jax.sharding import PartitionSpec as P

HEAD_DIM = 128


def head_pass(query_head, key_head, value_head, grad_head, key_mask):
    inv_root = 1.0 / math.sqrt(query_head.shape[1])
    scores = jnp.dot(query_head, key_head.T, preferred_element_type=jnp.float32) * inv_root
    scores = jnp.where(key_mask, scores, -1e30)
    highest = jnp.max(scores, axis=1, keepdims=True)
    weights = jnp.exp(scores - highest)
    row_total = jnp.sum(weights, axis=1, keepdims=True)
    weights_bf = (weights / row_total).astype(jnp.bfloat16)
    result = jnp.dot(weights_bf, value_head, preferred_element_type=jnp.float32).astype(
        jnp.bfloat16
    )
    grad_weights = jnp.dot(grad_head, value_head.T, preferred_element_type=jnp.float32)
    row_dot = jnp.sum(
        grad_head.astype(jnp.float32) * result.astype(jnp.float32), axis=1, keepdims=True
    )
    grad_scores = (weights_bf.astype(jnp.float32) * (grad_weights - row_dot)).astype(jnp.bfloat16)
    grad_query = (
        jnp.dot(grad_scores, key_head, preferred_element_type=jnp.float32) * inv_root
    ).astype(jnp.bfloat16)
    return (result, grad_query)


def per_device(
    queries, mem_keys, mem_values, lengths, mates, out_grad, mlp_input, gate_pre, hidden_grad
):
    members = lax.axis_size("grp")
    rows_q = queries.shape[2]
    mem_rows = mem_keys.shape[2]
    heads_all = queries.shape[3] // HEAD_DIM
    local_heads = heads_all // members
    docs_block = max(1, min(members, 512 // rows_q))
    block_count = members // docs_block
    row_count = docs_block * rows_q
    allowed = (mates[0] > 0) | jnp.eye(members, dtype=bool)
    live_keys = jnp.arange(mem_rows, dtype=jnp.int32)[None, :] < lengths[0][:, None]

    def split_heads(block):
        return block[0, 0].reshape(block.shape[2], members, local_heads, HEAD_DIM)

    def per_head(pieces):
        query_head, key_head, value_head, grad_head = pieces

        def block_step(block_num):
            first_row = block_num * row_count
            query_rows = lax.dynamic_slice_in_dim(query_head, first_row, row_count, 0)
            grad_rows = lax.dynamic_slice_in_dim(grad_head, first_row, row_count, 0)
            allowed_rows = lax.dynamic_slice_in_dim(allowed, block_num * docs_block, docs_block, 0)
            key_mask = jnp.broadcast_to(
                allowed_rows[:, None, :, None] & live_keys[None, None, :, :],
                (docs_block, rows_q, members, mem_rows),
            )
            key_mask = key_mask.reshape(row_count, members * mem_rows)
            return head_pass(query_rows, key_head, value_head, grad_rows, key_mask)

        results, gradients = lax.map(block_step, jnp.arange(block_count))
        return (
            results.reshape(members * rows_q, HEAD_DIM),
            gradients.reshape(members * rows_q, HEAD_DIM),
        )

    exchanged = (
        lax.all_to_all(split_heads(queries), "grp", split_axis=1, concat_axis=0, tiled=True),
        lax.all_to_all(split_heads(mem_keys), "grp", split_axis=1, concat_axis=0, tiled=True),
        lax.all_to_all(split_heads(mem_values), "grp", split_axis=1, concat_axis=0, tiled=True),
        lax.all_to_all(split_heads(out_grad), "grp", split_axis=1, concat_axis=0, tiled=True),
    )
    query_all, key_all, value_all, grad_all = [
        jnp.moveaxis(member[:, 0], 1, 0) for member in exchanged
    ]
    results, gradients = lax.map(per_head, (query_all, key_all, value_all, grad_all))
    heads_out = jnp.moveaxis(results, 0, 1)[:, None]
    heads_grad = jnp.moveaxis(gradients, 0, 1)[:, None]
    back_out, back_grad = (
        lax.all_to_all(heads_out, "grp", split_axis=0, concat_axis=1, tiled=True),
        lax.all_to_all(heads_grad, "grp", split_axis=0, concat_axis=1, tiled=True),
    )
    attn_out = back_out.reshape(1, 1, rows_q, heads_all * HEAD_DIM)
    q_grad = back_grad.reshape(1, 1, rows_q, heads_all * HEAD_DIM)
    up_cot = (
        hidden_grad[0, 0].astype(jnp.float32) * jax.nn.silu(gate_pre[0, 0].astype(jnp.float32))
    ).astype(jnp.bfloat16)
    tokens = mlp_input[0, 0]
    contract = (((0,), (0,)), ((), ()))
    slices = lax.all_to_all(up_cot, "grp", split_axis=1, concat_axis=0, tiled=True)
    partial_value = lax.dot_general(
        lax.all_gather(tokens, "grp", axis=0, tiled=True),
        slices,
        contract,
        preferred_element_type=jnp.float32,
    )
    up_grad = lax.psum_scatter(
        partial_value.astype(jnp.bfloat16), "dp", scatter_dimension=1, tiled=True
    ).astype(jnp.float32)
    return (attn_out, q_grad, up_grad)


MESH = pl.DeviceIdType.MESH
F32 = jnp.float32
BF16 = jnp.bfloat16
WIDTH = 512


def fused_kernel(
    nz,
    mask_ref, q_ref, k_ref, v_ref, g_ref, x_ref, ct_ref,
    attn_ref, qgrad_ref, up_ref,
    xall, ctall, qb, kb, vb, gb, res, back, outgo, income,
    x_send, x_recv, c_send, c_recv, a_send, a_recv, b_send, b_recv, z_send, z_recv,
):
    grp = lax.axis_index("grp")
    dp = lax.axis_index("dp")
    y, c = grp // 2, lax.rem(grp, 2)
    z, x = dp // 2, lax.rem(dp, 2)
    rows = x_ref.shape[0]
    chunks = xall.shape[0]
    members = qb.shape[0]
    span = qb.shape[2]
    heads = span // HEAD_DIM
    mem_rows = kb.shape[1]
    inv_root = 1.0 / math.sqrt(HEAD_DIM)

    def device(zz, xx, yy, cc):
        return {"dp": zz * 2 + xx, "grp": yy * 2 + cc}

    def block(xx, yy, cc):
        return xx * 4 + yy * 2 + cc

    def peer(r):
        px = lax.rem(x + r // 4, 2)
        py = lax.rem(y + lax.rem(r // 2, 2), 2)
        pc = lax.rem(c + lax.rem(r, 2), 2)
        return px, py, pc

    barrier = pltpu.get_barrier_semaphore()
    for r in range(1, 8):
        pl.semaphore_signal(barrier, inc=1, device_id=device(z, *peer(r)), device_id_type=MESH)

    @pl.when(z > 0)
    def _():
        pl.semaphore_signal(barrier, inc=1, device_id=device(z - 1, x, y, c), device_id_type=MESH)

    @pl.when(z < nz - 1)
    def _():
        pl.semaphore_signal(barrier, inc=1, device_id=device(z + 1, x, y, c), device_id_type=MESH)

    mine = block(x, y, c)

    def rows_of(b):
        return pl.ds(pl.multiple_of(b * rows, rows), rows)

    def cols_of(k, width):
        return pl.ds(pl.multiple_of(k * width, width), width)

    sib = device(z, x, y, 1 - c)
    xdev = device(z, 1 - x, y, c)
    ydev = device(z, x, 1 - y, c)
    own_b = mine
    x_b = block(1 - x, y, c)
    y_b = block(x, 1 - y, c)
    d_b = block(1 - x, 1 - y, c)

    def own_copy(k, role, dev):
        return pltpu.make_async_remote_copy(
            src_ref=x_ref.at[:, cols_of(k, WIDTH)],
            dst_ref=xall.at[k, rows_of(own_b)],
            send_sem=x_send.at[k, role], recv_sem=x_recv.at[k, role],
            device_id=dev, device_id_type=MESH,
        )

    def relay_copy(k, role, b, dev):
        return pltpu.make_async_remote_copy(
            src_ref=xall.at[k, rows_of(b)],
            dst_ref=xall.at[k, rows_of(b)],
            send_sem=x_send.at[k, role], recv_sem=x_recv.at[k, role],
            device_id=dev, device_id_type=MESH,
        )

    def x_copies(k):
        return [
            own_copy(k, 0, xdev), own_copy(k, 1, ydev), relay_copy(k, 2, y_b, xdev),
            own_copy(k, 3, sib), relay_copy(k, 4, x_b, sib), relay_copy(k, 5, y_b, sib),
            relay_copy(k, 6, d_b, sib),
        ]

    def start_own(k):
        cs = x_copies(k)
        cs[1].start()
        cs[0].start()
        cs[3].start()

    def relay(k):
        cs = x_copies(k)
        cs[1].wait_recv()
        cs[2].start()
        cs[5].start()
        cs[0].wait_recv()
        cs[4].start()
        cs[2].wait_recv()
        cs[6].start()

    def ct_copy(t, r):
        px, py, pc = peer(r)
        return pltpu.make_async_remote_copy(
            src_ref=ct_ref.at[py * 2 + pc, t * 2 + px],
            dst_ref=ctall.at[t, :, rows_of(mine)],
            send_sem=c_send.at[t, r], recv_sem=c_recv.at[t, r],
            device_id=device(z, px, py, pc), device_id_type=MESH,
        )

    def ct_start(t):
        @pl.loop(1, 8)
        def _(r):
            ct_copy(t, r).start()

    def ct_wait(t):
        @pl.loop(1, 8)
        def _(r):
            ct_copy(t, r).wait_recv()

    half = nz // 2

    def dest(i):
        down = nz - 1 - i
        down = jnp.where(down <= z, down - 1, down)
        up = jnp.where(i >= z, i + 1, i)
        return jnp.where(z < half, down, up)

    def att_copy(a, src, dst, j):
        p = lax.rem(grp + j, members)
        return pltpu.make_async_remote_copy(
            src_ref=src.at[:, cols_of(p, span)],
            dst_ref=dst.at[grp],
            send_sem=a_send.at[a, j], recv_sem=a_recv.at[a, j],
            device_id={"dp": dp, "grp": p}, device_id_type=MESH,
        )

    pairs = ((q_ref, qb), (k_ref, kb), (v_ref, vb), (g_ref, gb))

    def att_start(which):
        for a in which:
            for j in range(1, members):
                att_copy(a, *pairs[a], j).start()

    def back_copy(h, o, j):
        p = lax.rem(grp + j, members)
        return pltpu.make_async_remote_copy(
            src_ref=res.at[h, o, p], dst_ref=back.at[h, o, grp],
            send_sem=b_send.at[h, o, j], recv_sem=b_recv.at[h, o, j],
            device_id={"dp": dp, "grp": p}, device_id_type=MESH,
        )

    def head(h):
        cols = cols_of(h, HEAD_DIM)
        nt = (((1,), (1,)), ((), ()))
        kh = kb[:, :, cols].reshape(members * mem_rows, HEAD_DIM)
        vh = vb[:, :, cols].reshape(members * mem_rows, HEAD_DIM)

        @pl.loop(0, members)
        def _(m):
            qh = qb[m, :, cols]
            gh = gb[m, :, cols]
            s = lax.dot_general(qh, kh, nt, preferred_element_type=F32) * inv_root
            s = jnp.where(mask_ref[m] > 0, s, -1e30)
            w = jnp.exp(s - jnp.max(s, axis=1, keepdims=True))
            p = (w / jnp.sum(w, axis=1, keepdims=True)).astype(BF16)
            o = jnp.dot(p, vh, preferred_element_type=F32).astype(BF16)
            gp = lax.dot_general(gh, vh, nt, preferred_element_type=F32)
            rd = jnp.sum(gh.astype(F32) * o.astype(F32), axis=1, keepdims=True)
            gs = (p.astype(F32) * (gp - rd)).astype(BF16)
            res[h, 0, m] = o
            res[h, 1, m] = (jnp.dot(gs, kh, preferred_element_type=F32) * inv_root).astype(BF16)

        for o in range(2):
            for j in range(1, members):
                back_copy(h, o, j).start()

    def z_copy(t, k):
        right = t > z
        nxt = jnp.where(right, z + 1, z - 1)
        nxt = jnp.minimum(jnp.maximum(nxt, 0), nz - 1)
        slot = jnp.where(jnp.logical_and(nxt == t, t < z), nz, t)
        return pltpu.make_async_remote_copy(
            src_ref=outgo.at[t, k], dst_ref=income.at[slot, k],
            send_sem=z_send.at[t, k], recv_sem=z_recv.at[slot, k],
            device_id=device(nxt, x, y, c), device_id_type=MESH,
        )

    def z_wait(slot, k):
        pltpu.make_async_remote_copy(
            src_ref=income.at[slot, k], dst_ref=income.at[slot, k],
            send_sem=z_send.at[0, k], recv_sem=z_recv.at[slot, k],
            device_id=sib, device_id_type=MESH,
        ).wait_recv()

    def part(t, k):
        return jnp.dot(ctall[t], xall[k], preferred_element_type=F32)

    def push(k):
        @pl.loop(0, nz - 1)
        def _(i):
            t = dest(i)

            @pl.when(k == 0)
            def _():
                ct_wait(t)

            value = part(t, k)
            has = jnp.where(t > z, z > 0, z < nz - 1)

            @pl.when(has)
            def _():
                z_wait(t, k)
                outgo[t, k] = (value + income[t, k].astype(F32)).astype(BF16)

            @pl.when(jnp.logical_not(has))
            def _():
                outgo[t, k] = value.astype(BF16)

            z_copy(t, k).start()

    def finish(k):
        cols = cols_of(k, WIDTH)
        up_ref[:, cols] = part(z, k)

        @pl.when(z > 0)
        def _():
            z_wait(z, k)
            up_ref[:, cols] += income[z, k].astype(F32)

        @pl.when(z < nz - 1)
        def _():
            z_wait(nz, k)
            up_ref[:, cols] += income[nz, k].astype(F32)

    for t in range(nz):
        ctall[t, :, rows_of(mine)] = ct_ref[grp, t * 2 + x]
    for k in range(chunks):
        xall[k, rows_of(mine)] = x_ref[:, k * WIDTH : (k + 1) * WIDTH]
    for src, dst in pairs:
        dst[grp] = src[:, cols_of(grp, span)]

    others = 7 + jnp.where(z > 0, 1, 0) + jnp.where(z < nz - 1, 1, 0)
    pl.semaphore_wait(barrier, others)

    ct_start(dest(0))
    start_own(0)

    @pl.loop(1, nz - 1)
    def _(i):
        ct_start(dest(i))

    start_own(1)
    ct_start(z)
    relay(0)

    first_head = 3
    lag = 3

    @pl.loop(0, chunks)
    def _(k):
        for role in range(3, 7):
            x_copies(k)[role].wait_recv()
        push(k)

        @pl.when(k + 2 < chunks)
        def _():
            start_own(k + 2)

        @pl.when(k == 0)
        def _():
            att_start((0, 1))

        @pl.when(k == 1)
        def _():
            att_start((2, 3))

        @pl.when(k + 1 < chunks)
        def _():
            relay(k + 1)

        @pl.when(k == first_head)
        def _():
            for a in range(4):
                for j in range(1, members):
                    att_copy(a, *pairs[a], j).wait_recv()

        @pl.when(jnp.logical_and(k >= first_head, k < first_head + heads))
        def _():
            head(k - first_head)

        @pl.when(k == lag)
        def _():
            ct_wait(z)

        @pl.when(k >= lag)
        def _():
            finish(k - lag)

    @pl.loop(chunks - lag, chunks)
    def _(k):
        finish(k)

    for o, ref in ((0, attn_ref), (1, qgrad_ref)):
        for h in range(heads):
            for j in range(1, members):
                back_copy(h, o, j).wait_recv()
                p = lax.rem(grp + members - j, members)
                ref[:, pl.ds(pl.multiple_of(p * span + h * HEAD_DIM, HEAD_DIM), HEAD_DIM)] = back[h, o, p]
            ref[:, pl.ds(pl.multiple_of(grp * span + h * HEAD_DIM, HEAD_DIM), HEAD_DIM)] = res[h, o, grp]

    @pl.loop(0, chunks)
    def _(k):
        for copy in x_copies(k):
            copy.wait_send()

        @pl.loop(0, nz - 1)
        def _(i):
            z_copy(dest(i), k).wait_send()

    @pl.loop(0, nz)
    def _(t):
        @pl.loop(1, 8)
        def _(r):
            ct_copy(t, r).wait_send()

    for a in range(4):
        for j in range(1, members):
            att_copy(a, *pairs[a], j).wait_send()

    @pl.loop(0, heads)
    def _(h):
        for o in range(2):
            for j in range(1, members):
                back_copy(h, o, j).wait_send()


def fused_call(
    nz, queries, mem_keys, mem_values, lengths, mates, out_grad, mlp_input, gate_pre, hidden_grad
):
    members = lax.axis_size("grp")
    groups = lax.axis_size("dp")
    rows, width = queries.shape[2:]
    mem_rows = mem_keys.shape[2]
    model, hidden = mlp_input.shape[3], gate_pre.shape[3]
    span = width // members
    heads = span // HEAD_DIM
    own = hidden // (members * groups)
    layer = 2 * members
    chunks = model // WIDTH
    up_cot = (
        hidden_grad[0, 0].astype(F32) * jax.nn.silu(gate_pre[0, 0].astype(F32))
    ).astype(BF16)
    ct = up_cot.T.reshape(members, groups, own, rows)
    allowed = (mates[0] > 0) | jnp.eye(members, dtype=bool)
    live = jnp.arange(mem_rows, dtype=jnp.int32)[None, :] < lengths[0][:, None]
    mask = (allowed[:, :, None] & live[None]).astype(F32).reshape(members, 1, members * mem_rows)
    vm = pl.BlockSpec(memory_space=pltpu.VMEM)
    dma = pltpu.SemaphoreType.DMA
    attn, qgrad, up = pl.pallas_call(
        functools.partial(fused_kernel, nz),
        out_shape=(
            jax.ShapeDtypeStruct((rows, width), BF16),
            jax.ShapeDtypeStruct((rows, width), BF16),
            jax.ShapeDtypeStruct((own, model), F32),
        ),
        in_specs=[vm] * 7,
        out_specs=(vm, vm, vm),
        scratch_shapes=[
            pltpu.VMEM((chunks, layer * rows, WIDTH), BF16),
            pltpu.VMEM((nz, own, layer * rows), BF16),
            pltpu.VMEM((members, rows, span), BF16),
            pltpu.VMEM((members, mem_rows, span), BF16),
            pltpu.VMEM((members, mem_rows, span), BF16),
            pltpu.VMEM((members, rows, span), BF16),
            pltpu.VMEM((heads, 2, members, rows, HEAD_DIM), BF16),
            pltpu.VMEM((heads, 2, members, rows, HEAD_DIM), BF16),
            pltpu.VMEM((nz, chunks, own, WIDTH), BF16),
            pltpu.VMEM((nz + 1, chunks, own, WIDTH), BF16),
            dma((chunks, 7)), dma((chunks, 7)),
            dma((nz, 8)), dma((nz, 8)),
            dma((4, members)), dma((4, members)),
            dma((heads, 2, members)), dma((heads, 2, members)),
            dma((nz, chunks)), dma((nz + 1, chunks)),
        ],
        compiler_params=pltpu.CompilerParams(
            collective_id=0, has_side_effects=True, vmem_limit_bytes=60 * 1024 * 1024
        ),
        name="fused",
    )(
        mask, queries[0, 0], mem_keys[0, 0], mem_values[0, 0], out_grad[0, 0], mlp_input[0, 0], ct
    )
    return attn[None, None], qgrad[None, None], up.T


def choose(*args):
    members, groups = lax.axis_size("grp"), lax.axis_size("dp")
    near = 1 << ((groups.bit_length() - 1) // 2)
    hidden, model = args[7].shape[3], args[6].shape[3]
    own = hidden // (members * groups)
    fits = members == 4 and near == 2 and groups % 2 == 0 and own % 16 == 0 and model % WIDTH == 0
    if fits and model // WIDTH >= 3 + args[0].shape[3] // members // HEAD_DIM:
        return fused_call(groups // near, *args)
    return per_device(*args)


def solution(mesh):
    return jax.shard_map(
        choose,
        mesh=mesh,
        in_specs=(
            P("dp", "grp", None, None),
            P("dp", "grp", None, None),
            P("dp", "grp", None, None),
            P("dp", None),
            P("dp", None, None),
            P("dp", "grp", None, None),
            P("dp", "grp", None, None),
            P("dp", "grp", None, None),
            P("dp", "grp", None, None),
        ),
        out_specs=(P("dp", "grp", None, None), P("dp", "grp", None, None), P(None, ("grp", "dp"))),
        check_vma=False,
    )
```

```python
import functools
import math

import jax
import jax.numpy as jnp
from jax import lax
from jax.experimental import pallas as pl
from jax.experimental.pallas import tpu as pltpu
from jax.sharding import PartitionSpec as P

HEAD_DIM = 128


def head_pass(query_head, key_head, value_head, grad_head, key_mask):
    inv_root = 1.0 / math.sqrt(query_head.shape[1])
    scores = jnp.dot(query_head, key_head.T, preferred_element_type=jnp.float32) * inv_root
    scores = jnp.where(key_mask, scores, -1e30)
    highest = jnp.max(scores, axis=1, keepdims=True)
    weights = jnp.exp(scores - highest)
    row_total = jnp.sum(weights, axis=1, keepdims=True)
    weights_bf = (weights / row_total).astype(jnp.bfloat16)
    result = jnp.dot(weights_bf, value_head, preferred_element_type=jnp.float32).astype(
        jnp.bfloat16
    )
    grad_weights = jnp.dot(grad_head, value_head.T, preferred_element_type=jnp.float32)
    row_dot = jnp.sum(
        grad_head.astype(jnp.float32) * result.astype(jnp.float32), axis=1, keepdims=True
    )
    grad_scores = (weights_bf.astype(jnp.float32) * (grad_weights - row_dot)).astype(jnp.bfloat16)
    grad_query = (
        jnp.dot(grad_scores, key_head, preferred_element_type=jnp.float32) * inv_root
    ).astype(jnp.bfloat16)
    return (result, grad_query)


def per_device(
    queries, mem_keys, mem_values, lengths, mates, out_grad, mlp_input, gate_pre, hidden_grad
):
    members = lax.axis_size("grp")
    rows_q = queries.shape[2]
    mem_rows = mem_keys.shape[2]
    heads_all = queries.shape[3] // HEAD_DIM
    local_heads = heads_all // members
    docs_block = max(1, min(members, 512 // rows_q))
    block_count = members // docs_block
    row_count = docs_block * rows_q
    allowed = (mates[0] > 0) | jnp.eye(members, dtype=bool)
    live_keys = jnp.arange(mem_rows, dtype=jnp.int32)[None, :] < lengths[0][:, None]

    def split_heads(block):
        return block[0, 0].reshape(block.shape[2], members, local_heads, HEAD_DIM)

    def per_head(pieces):
        query_head, key_head, value_head, grad_head = pieces

        def block_step(block_num):
            first_row = block_num * row_count
            query_rows = lax.dynamic_slice_in_dim(query_head, first_row, row_count, 0)
            grad_rows = lax.dynamic_slice_in_dim(grad_head, first_row, row_count, 0)
            allowed_rows = lax.dynamic_slice_in_dim(allowed, block_num * docs_block, docs_block, 0)
            key_mask = jnp.broadcast_to(
                allowed_rows[:, None, :, None] & live_keys[None, None, :, :],
                (docs_block, rows_q, members, mem_rows),
            )
            key_mask = key_mask.reshape(row_count, members * mem_rows)
            return head_pass(query_rows, key_head, value_head, grad_rows, key_mask)

        results, gradients = lax.map(block_step, jnp.arange(block_count))
        return (
            results.reshape(members * rows_q, HEAD_DIM),
            gradients.reshape(members * rows_q, HEAD_DIM),
        )

    exchanged = (
        lax.all_to_all(split_heads(queries), "grp", split_axis=1, concat_axis=0, tiled=True),
        lax.all_to_all(split_heads(mem_keys), "grp", split_axis=1, concat_axis=0, tiled=True),
        lax.all_to_all(split_heads(mem_values), "grp", split_axis=1, concat_axis=0, tiled=True),
        lax.all_to_all(split_heads(out_grad), "grp", split_axis=1, concat_axis=0, tiled=True),
    )
    query_all, key_all, value_all, grad_all = [
        jnp.moveaxis(member[:, 0], 1, 0) for member in exchanged
    ]
    results, gradients = lax.map(per_head, (query_all, key_all, value_all, grad_all))
    heads_out = jnp.moveaxis(results, 0, 1)[:, None]
    heads_grad = jnp.moveaxis(gradients, 0, 1)[:, None]
    back_out, back_grad = (
        lax.all_to_all(heads_out, "grp", split_axis=0, concat_axis=1, tiled=True),
        lax.all_to_all(heads_grad, "grp", split_axis=0, concat_axis=1, tiled=True),
    )
    attn_out = back_out.reshape(1, 1, rows_q, heads_all * HEAD_DIM)
    q_grad = back_grad.reshape(1, 1, rows_q, heads_all * HEAD_DIM)
    up_cot = (
        hidden_grad[0, 0].astype(jnp.float32) * jax.nn.silu(gate_pre[0, 0].astype(jnp.float32))
    ).astype(jnp.bfloat16)
    tokens = mlp_input[0, 0]
    contract = (((0,), (0,)), ((), ()))
    slices = lax.all_to_all(up_cot, "grp", split_axis=1, concat_axis=0, tiled=True)
    partial_value = lax.dot_general(
        lax.all_gather(tokens, "grp", axis=0, tiled=True),
        slices,
        contract,
        preferred_element_type=jnp.float32,
    )
    up_grad = lax.psum_scatter(
        partial_value.astype(jnp.bfloat16), "dp", scatter_dimension=1, tiled=True
    ).astype(jnp.float32)
    return (attn_out, q_grad, up_grad)


MESH = pl.DeviceIdType.MESH
F32 = jnp.float32
BF16 = jnp.bfloat16
WIDTH = 512


def fused_kernel(
    nz,
    mask_ref, q_ref, k_ref, v_ref, g_ref, x_ref, ct_ref,
    attn_ref, qgrad_ref, up_ref,
    xall, ctall, qb, kb, vb, gb, res, back, outgo, income,
    x_send, x_recv, c_send, c_recv, a_send, a_recv, b_send, b_recv, z_send, z_recv,
):
    grp = lax.axis_index("grp")
    dp = lax.axis_index("dp")
    y, c = grp // 2, lax.rem(grp, 2)
    z, x = dp // 2, lax.rem(dp, 2)
    rows = x_ref.shape[0]
    chunks = xall.shape[0]
    members = qb.shape[0]
    span = qb.shape[2]
    heads = span // HEAD_DIM
    mem_rows = kb.shape[1]
    inv_root = 1.0 / math.sqrt(HEAD_DIM)

    def device(zz, xx, yy, cc):
        return {"dp": zz * 2 + xx, "grp": yy * 2 + cc}

    def block(xx, yy, cc):
        return xx * 4 + yy * 2 + cc

    def peer(r):
        px = lax.rem(x + r // 4, 2)
        py = lax.rem(y + lax.rem(r // 2, 2), 2)
        pc = lax.rem(c + lax.rem(r, 2), 2)
        return px, py, pc

    barrier = pltpu.get_barrier_semaphore()
    for r in range(1, 8):
        pl.semaphore_signal(barrier, inc=1, device_id=device(z, *peer(r)), device_id_type=MESH)

    @pl.when(z > 0)
    def _():
        pl.semaphore_signal(barrier, inc=1, device_id=device(z - 1, x, y, c), device_id_type=MESH)

    @pl.when(z < nz - 1)
    def _():
        pl.semaphore_signal(barrier, inc=1, device_id=device(z + 1, x, y, c), device_id_type=MESH)

    mine = block(x, y, c)

    def rows_of(b):
        return pl.ds(pl.multiple_of(b * rows, rows), rows)

    def cols_of(k, width):
        return pl.ds(pl.multiple_of(k * width, width), width)

    sib = device(z, x, y, 1 - c)
    xdev = device(z, 1 - x, y, c)
    ydev = device(z, x, 1 - y, c)
    own_b = mine
    x_b = block(1 - x, y, c)
    y_b = block(x, 1 - y, c)
    d_b = block(1 - x, 1 - y, c)

    def own_copy(k, role, dev):
        return pltpu.make_async_remote_copy(
            src_ref=x_ref.at[:, cols_of(k, WIDTH)],
            dst_ref=xall.at[k, rows_of(own_b)],
            send_sem=x_send.at[k, role], recv_sem=x_recv.at[k, role],
            device_id=dev, device_id_type=MESH,
        )

    def relay_copy(k, role, b, dev):
        return pltpu.make_async_remote_copy(
            src_ref=xall.at[k, rows_of(b)],
            dst_ref=xall.at[k, rows_of(b)],
            send_sem=x_send.at[k, role], recv_sem=x_recv.at[k, role],
            device_id=dev, device_id_type=MESH,
        )

    def x_copies(k):
        return [
            own_copy(k, 0, xdev), own_copy(k, 1, ydev), relay_copy(k, 2, y_b, xdev),
            own_copy(k, 3, sib), relay_copy(k, 4, x_b, sib), relay_copy(k, 5, y_b, sib),
            relay_copy(k, 6, d_b, sib),
        ]

    def start_own(k):
        cs = x_copies(k)
        cs[1].start()
        cs[0].start()
        cs[3].start()

    def relay_far(k):
        cs = x_copies(k)
        cs[1].wait_recv()
        cs[2].start()
        cs[5].start()
        cs[0].wait_recv()
        cs[4].start()

    def relay_near(k):
        cs = x_copies(k)
        cs[2].wait_recv()
        cs[6].start()

    def ct_copy(t, r):
        px, py, pc = peer(r)
        return pltpu.make_async_remote_copy(
            src_ref=ct_ref.at[py * 2 + pc, t * 2 + px],
            dst_ref=ctall.at[t, :, rows_of(mine)],
            send_sem=c_send.at[t, r], recv_sem=c_recv.at[t, r],
            device_id=device(z, px, py, pc), device_id_type=MESH,
        )

    def ct_start(t):
        @pl.loop(1, 8)
        def _(r):
            ct_copy(t, r).start()

    def ct_wait(t):
        @pl.loop(1, 8)
        def _(r):
            ct_copy(t, r).wait_recv()

    half = nz // 2

    def dest(i):
        down = nz - 1 - i
        down = jnp.where(down <= z, down - 1, down)
        up = jnp.where(i >= z, i + 1, i)
        return jnp.where(z < half, down, up)

    def att_copy(a, src, dst, j):
        p = lax.rem(grp + j, members)
        return pltpu.make_async_remote_copy(
            src_ref=src.at[:, cols_of(p, span)],
            dst_ref=dst.at[grp],
            send_sem=a_send.at[a, j], recv_sem=a_recv.at[a, j],
            device_id={"dp": dp, "grp": p}, device_id_type=MESH,
        )

    pairs = ((q_ref, qb), (k_ref, kb), (v_ref, vb), (g_ref, gb))

    def att_start(which):
        for a in which:
            for j in range(1, members):
                att_copy(a, *pairs[a], j).start()

    def back_copy(h, o, j):
        p = lax.rem(grp + j, members)
        return pltpu.make_async_remote_copy(
            src_ref=res.at[h, o, p], dst_ref=back.at[h, o, grp],
            send_sem=b_send.at[h, o, j], recv_sem=b_recv.at[h, o, j],
            device_id={"dp": dp, "grp": p}, device_id_type=MESH,
        )

    def head(h):
        cols = cols_of(h, HEAD_DIM)
        nt = (((1,), (1,)), ((), ()))
        kh = kb[:, :, cols].reshape(members * mem_rows, HEAD_DIM)
        vh = vb[:, :, cols].reshape(members * mem_rows, HEAD_DIM)

        @pl.loop(0, members)
        def _(m):
            qh = qb[m, :, cols]
            gh = gb[m, :, cols]
            s = lax.dot_general(qh, kh, nt, preferred_element_type=F32) * inv_root
            s = jnp.where(mask_ref[m] > 0, s, -1e30)
            w = jnp.exp(s - jnp.max(s, axis=1, keepdims=True))
            p = (w / jnp.sum(w, axis=1, keepdims=True)).astype(BF16)
            o = jnp.dot(p, vh, preferred_element_type=F32).astype(BF16)
            gp = lax.dot_general(gh, vh, nt, preferred_element_type=F32)
            rd = jnp.sum(gh.astype(F32) * o.astype(F32), axis=1, keepdims=True)
            gs = (p.astype(F32) * (gp - rd)).astype(BF16)
            res[h, 0, m] = o
            res[h, 1, m] = (jnp.dot(gs, kh, preferred_element_type=F32) * inv_root).astype(BF16)

        for o in range(2):
            for j in range(1, members):
                back_copy(h, o, j).start()

    def z_copy(t, k):
        right = t > z
        nxt = jnp.where(right, z + 1, z - 1)
        nxt = jnp.minimum(jnp.maximum(nxt, 0), nz - 1)
        slot = jnp.where(jnp.logical_and(nxt == t, t < z), nz, t)
        return pltpu.make_async_remote_copy(
            src_ref=outgo.at[t, k], dst_ref=income.at[slot, k],
            send_sem=z_send.at[t, k], recv_sem=z_recv.at[slot, k],
            device_id=device(nxt, x, y, c), device_id_type=MESH,
        )

    def z_wait(slot, k):
        pltpu.make_async_remote_copy(
            src_ref=income.at[slot, k], dst_ref=income.at[slot, k],
            send_sem=z_send.at[0, k], recv_sem=z_recv.at[slot, k],
            device_id=sib, device_id_type=MESH,
        ).wait_recv()

    def part(t, k):
        return jnp.dot(ctall[t], xall[k], preferred_element_type=F32)

    def push(k):
        @pl.loop(0, nz - 1)
        def _(i):
            t = dest(i)

            @pl.when(k == 0)
            def _():
                ct_wait(t)

            value = part(t, k)
            has = jnp.where(t > z, z > 0, z < nz - 1)

            @pl.when(has)
            def _():
                z_wait(t, k)
                outgo[t, k] = (value + income[t, k].astype(F32)).astype(BF16)

            @pl.when(jnp.logical_not(has))
            def _():
                outgo[t, k] = value.astype(BF16)

            z_copy(t, k).start()

    def finish(k):
        cols = cols_of(k, WIDTH)
        up_ref[:, cols] = part(z, k)

        @pl.when(z > 0)
        def _():
            z_wait(z, k)
            up_ref[:, cols] += income[z, k].astype(F32)

        @pl.when(z < nz - 1)
        def _():
            z_wait(nz, k)
            up_ref[:, cols] += income[nz, k].astype(F32)

    for t in range(nz):
        ctall[t, :, rows_of(mine)] = ct_ref[grp, t * 2 + x]
    for k in range(chunks):
        xall[k, rows_of(mine)] = x_ref[:, k * WIDTH : (k + 1) * WIDTH]
    for src, dst in pairs:
        dst[grp] = src[:, cols_of(grp, span)]

    others = 7 + jnp.where(z > 0, 1, 0) + jnp.where(z < nz - 1, 1, 0)
    pl.semaphore_wait(barrier, others)

    ct_start(dest(0))
    start_own(0)
    ct_start(dest(1))
    relay_far(0)
    start_own(1)

    @pl.loop(2, nz - 1)
    def _(i):
        ct_start(dest(i))

    relay_near(0)
    relay_far(1)
    start_own(2)

    first_head = 4
    lag = 3

    @pl.loop(0, chunks)
    def _(k):
        for role in range(3, 7):
            x_copies(k)[role].wait_recv()
        push(k)

        @pl.when(k + 1 < chunks)
        def _():
            relay_near(k + 1)

        @pl.when(k + 2 < chunks)
        def _():
            relay_far(k + 2)

        @pl.when(k + 3 < chunks)
        def _():
            start_own(k + 3)

        @pl.when(k == 0)
        def _():
            ct_start(z)
            att_start((0, 1))

        @pl.when(k == 1)
        def _():
            att_start((2, 3))

        @pl.when(k == first_head)
        def _():
            for a in range(4):
                for j in range(1, members):
                    att_copy(a, *pairs[a], j).wait_recv()

        @pl.when(jnp.logical_and(k >= first_head, k < first_head + heads))
        def _():
            head(k - first_head)

        @pl.when(k == lag)
        def _():
            ct_wait(z)

        @pl.when(k >= lag)
        def _():
            finish(k - lag)

    @pl.loop(chunks - lag, chunks)
    def _(k):
        finish(k)

    for o, ref in ((0, attn_ref), (1, qgrad_ref)):
        for h in range(heads):
            for j in range(1, members):
                back_copy(h, o, j).wait_recv()
                p = lax.rem(grp + members - j, members)
                ref[:, pl.ds(pl.multiple_of(p * span + h * HEAD_DIM, HEAD_DIM), HEAD_DIM)] = back[h, o, p]
            ref[:, pl.ds(pl.multiple_of(grp * span + h * HEAD_DIM, HEAD_DIM), HEAD_DIM)] = res[h, o, grp]

    @pl.loop(0, chunks)
    def _(k):
        for copy in x_copies(k):
            copy.wait_send()

        @pl.loop(0, nz - 1)
        def _(i):
            z_copy(dest(i), k).wait_send()

    @pl.loop(0, nz)
    def _(t):
        @pl.loop(1, 8)
        def _(r):
            ct_copy(t, r).wait_send()

    for a in range(4):
        for j in range(1, members):
            att_copy(a, *pairs[a], j).wait_send()

    @pl.loop(0, heads)
    def _(h):
        for o in range(2):
            for j in range(1, members):
                back_copy(h, o, j).wait_send()


def fused_call(
    nz, queries, mem_keys, mem_values, lengths, mates, out_grad, mlp_input, gate_pre, hidden_grad
):
    members = lax.axis_size("grp")
    groups = lax.axis_size("dp")
    rows, width = queries.shape[2:]
    mem_rows = mem_keys.shape[2]
    model, hidden = mlp_input.shape[3], gate_pre.shape[3]
    span = width // members
    heads = span // HEAD_DIM
    own = hidden // (members * groups)
    layer = 2 * members
    chunks = model // WIDTH
    up_cot = (
        hidden_grad[0, 0].astype(F32) * jax.nn.silu(gate_pre[0, 0].astype(F32))
    ).astype(BF16)
    ct = up_cot.T.reshape(members, groups, own, rows)
    allowed = (mates[0] > 0) | jnp.eye(members, dtype=bool)
    live = jnp.arange(mem_rows, dtype=jnp.int32)[None, :] < lengths[0][:, None]
    mask = (allowed[:, :, None] & live[None]).astype(F32).reshape(members, 1, members * mem_rows)
    vm = pl.BlockSpec(memory_space=pltpu.VMEM)
    dma = pltpu.SemaphoreType.DMA
    attn, qgrad, up = pl.pallas_call(
        functools.partial(fused_kernel, nz),
        out_shape=(
            jax.ShapeDtypeStruct((rows, width), BF16),
            jax.ShapeDtypeStruct((rows, width), BF16),
            jax.ShapeDtypeStruct((own, model), F32),
        ),
        in_specs=[vm] * 7,
        out_specs=(vm, vm, vm),
        scratch_shapes=[
            pltpu.VMEM((chunks, layer * rows, WIDTH), BF16),
            pltpu.VMEM((nz, own, layer * rows), BF16),
            pltpu.VMEM((members, rows, span), BF16),
            pltpu.VMEM((members, mem_rows, span), BF16),
            pltpu.VMEM((members, mem_rows, span), BF16),
            pltpu.VMEM((members, rows, span), BF16),
            pltpu.VMEM((heads, 2, members, rows, HEAD_DIM), BF16),
            pltpu.VMEM((heads, 2, members, rows, HEAD_DIM), BF16),
            pltpu.VMEM((nz, chunks, own, WIDTH), BF16),
            pltpu.VMEM((nz + 1, chunks, own, WIDTH), BF16),
            dma((chunks, 7)), dma((chunks, 7)),
            dma((nz, 8)), dma((nz, 8)),
            dma((4, members)), dma((4, members)),
            dma((heads, 2, members)), dma((heads, 2, members)),
            dma((nz, chunks)), dma((nz + 1, chunks)),
        ],
        compiler_params=pltpu.CompilerParams(
            collective_id=0, has_side_effects=True, vmem_limit_bytes=44 * 1024 * 1024
        ),
        name="fused",
    )(
        mask, queries[0, 0], mem_keys[0, 0], mem_values[0, 0], out_grad[0, 0], mlp_input[0, 0], ct
    )
    return attn[None, None], qgrad[None, None], up.T


def choose(*args):
    members, groups = lax.axis_size("grp"), lax.axis_size("dp")
    near = 1 << ((groups.bit_length() - 1) // 2)
    hidden, model = args[7].shape[3], args[6].shape[3]
    own = hidden // (members * groups)
    fits = members == 4 and near == 2 and groups % 2 == 0 and own % 16 == 0 and model % WIDTH == 0
    if fits and model // WIDTH >= 4 + args[0].shape[3] // members // HEAD_DIM:
        return fused_call(groups // near, *args)
    return per_device(*args)


def solution(mesh):
    return jax.shard_map(
        choose,
        mesh=mesh,
        in_specs=(
            P("dp", "grp", None, None),
            P("dp", "grp", None, None),
            P("dp", "grp", None, None),
            P("dp", None),
            P("dp", None, None),
            P("dp", "grp", None, None),
            P("dp", "grp", None, None),
            P("dp", "grp", None, None),
            P("dp", "grp", None, None),
        ),
        out_specs=(P("dp", "grp", None, None), P("dp", "grp", None, None), P(None, ("grp", "dp"))),
        check_vma=False,
    )
```

```python
import functools
import math

import jax
import jax.numpy as jnp
from jax import lax
from jax.experimental import pallas as pl
from jax.experimental.pallas import tpu as pltpu
from jax.sharding import PartitionSpec as P

HEAD_DIM = 128


def head_pass(query_head, key_head, value_head, grad_head, key_mask):
    inv_root = 1.0 / math.sqrt(query_head.shape[1])
    scores = jnp.dot(query_head, key_head.T, preferred_element_type=jnp.float32) * inv_root
    scores = jnp.where(key_mask, scores, -1e30)
    highest = jnp.max(scores, axis=1, keepdims=True)
    weights = jnp.exp(scores - highest)
    row_total = jnp.sum(weights, axis=1, keepdims=True)
    weights_bf = (weights / row_total).astype(jnp.bfloat16)
    result = jnp.dot(weights_bf, value_head, preferred_element_type=jnp.float32).astype(
        jnp.bfloat16
    )
    grad_weights = jnp.dot(grad_head, value_head.T, preferred_element_type=jnp.float32)
    row_dot = jnp.sum(
        grad_head.astype(jnp.float32) * result.astype(jnp.float32), axis=1, keepdims=True
    )
    grad_scores = (weights_bf.astype(jnp.float32) * (grad_weights - row_dot)).astype(jnp.bfloat16)
    grad_query = (
        jnp.dot(grad_scores, key_head, preferred_element_type=jnp.float32) * inv_root
    ).astype(jnp.bfloat16)
    return (result, grad_query)


def per_device(
    queries, mem_keys, mem_values, lengths, mates, out_grad, mlp_input, gate_pre, hidden_grad
):
    members = lax.axis_size("grp")
    rows_q = queries.shape[2]
    mem_rows = mem_keys.shape[2]
    heads_all = queries.shape[3] // HEAD_DIM
    local_heads = heads_all // members
    docs_block = max(1, min(members, 512 // rows_q))
    block_count = members // docs_block
    row_count = docs_block * rows_q
    allowed = (mates[0] > 0) | jnp.eye(members, dtype=bool)
    live_keys = jnp.arange(mem_rows, dtype=jnp.int32)[None, :] < lengths[0][:, None]

    def split_heads(block):
        return block[0, 0].reshape(block.shape[2], members, local_heads, HEAD_DIM)

    def per_head(pieces):
        query_head, key_head, value_head, grad_head = pieces

        def block_step(block_num):
            first_row = block_num * row_count
            query_rows = lax.dynamic_slice_in_dim(query_head, first_row, row_count, 0)
            grad_rows = lax.dynamic_slice_in_dim(grad_head, first_row, row_count, 0)
            allowed_rows = lax.dynamic_slice_in_dim(allowed, block_num * docs_block, docs_block, 0)
            key_mask = jnp.broadcast_to(
                allowed_rows[:, None, :, None] & live_keys[None, None, :, :],
                (docs_block, rows_q, members, mem_rows),
            )
            key_mask = key_mask.reshape(row_count, members * mem_rows)
            return head_pass(query_rows, key_head, value_head, grad_rows, key_mask)

        results, gradients = lax.map(block_step, jnp.arange(block_count))
        return (
            results.reshape(members * rows_q, HEAD_DIM),
            gradients.reshape(members * rows_q, HEAD_DIM),
        )

    exchanged = (
        lax.all_to_all(split_heads(queries), "grp", split_axis=1, concat_axis=0, tiled=True),
        lax.all_to_all(split_heads(mem_keys), "grp", split_axis=1, concat_axis=0, tiled=True),
        lax.all_to_all(split_heads(mem_values), "grp", split_axis=1, concat_axis=0, tiled=True),
        lax.all_to_all(split_heads(out_grad), "grp", split_axis=1, concat_axis=0, tiled=True),
    )
    query_all, key_all, value_all, grad_all = [
        jnp.moveaxis(member[:, 0], 1, 0) for member in exchanged
    ]
    results, gradients = lax.map(per_head, (query_all, key_all, value_all, grad_all))
    heads_out = jnp.moveaxis(results, 0, 1)[:, None]
    heads_grad = jnp.moveaxis(gradients, 0, 1)[:, None]
    back_out, back_grad = (
        lax.all_to_all(heads_out, "grp", split_axis=0, concat_axis=1, tiled=True),
        lax.all_to_all(heads_grad, "grp", split_axis=0, concat_axis=1, tiled=True),
    )
    attn_out = back_out.reshape(1, 1, rows_q, heads_all * HEAD_DIM)
    q_grad = back_grad.reshape(1, 1, rows_q, heads_all * HEAD_DIM)
    up_cot = (
        hidden_grad[0, 0].astype(jnp.float32) * jax.nn.silu(gate_pre[0, 0].astype(jnp.float32))
    ).astype(jnp.bfloat16)
    tokens = mlp_input[0, 0]
    contract = (((0,), (0,)), ((), ()))
    slices = lax.all_to_all(up_cot, "grp", split_axis=1, concat_axis=0, tiled=True)
    partial_value = lax.dot_general(
        lax.all_gather(tokens, "grp", axis=0, tiled=True),
        slices,
        contract,
        preferred_element_type=jnp.float32,
    )
    up_grad = lax.psum_scatter(
        partial_value.astype(jnp.bfloat16), "dp", scatter_dimension=1, tiled=True
    ).astype(jnp.float32)
    return (attn_out, q_grad, up_grad)


MESH = pl.DeviceIdType.MESH
F32 = jnp.float32
BF16 = jnp.bfloat16
WIDTH = 512


def fused_kernel(
    nz,
    mask_ref, q_ref, k_ref, v_ref, g_ref, x_ref, ct_ref,
    attn_ref, qgrad_ref, up_ref,
    xall, ctall, qb, kb, vb, gb, res, back, outgo, income,
    x_send, x_recv, c_send, c_recv, a_send, a_recv, b_send, b_recv, z_send, z_recv, l_sem,
):
    grp = lax.axis_index("grp")
    dp = lax.axis_index("dp")
    y, c = grp // 2, lax.rem(grp, 2)
    z, x = dp // 2, lax.rem(dp, 2)
    rows = x_ref.shape[0]
    chunks = xall.shape[0]
    members = qb.shape[0]
    span = qb.shape[2]
    heads = span // HEAD_DIM
    mem_rows = kb.shape[1]
    inv_root = 1.0 / math.sqrt(HEAD_DIM)

    def device(zz, xx, yy, cc):
        return {"dp": zz * 2 + xx, "grp": yy * 2 + cc}

    def block(xx, yy, cc):
        return xx * 4 + yy * 2 + cc

    def peer(r):
        px = lax.rem(x + r // 4, 2)
        py = lax.rem(y + lax.rem(r // 2, 2), 2)
        pc = lax.rem(c + lax.rem(r, 2), 2)
        return px, py, pc

    barrier = pltpu.get_barrier_semaphore()
    for r in range(1, 8):
        pl.semaphore_signal(barrier, inc=1, device_id=device(z, *peer(r)), device_id_type=MESH)

    @pl.when(z > 0)
    def _():
        pl.semaphore_signal(barrier, inc=1, device_id=device(z - 1, x, y, c), device_id_type=MESH)

    @pl.when(z < nz - 1)
    def _():
        pl.semaphore_signal(barrier, inc=1, device_id=device(z + 1, x, y, c), device_id_type=MESH)

    mine = block(x, y, c)

    def rows_of(b):
        return pl.ds(pl.multiple_of(b * rows, rows), rows)

    def cols_of(k, width):
        return pl.ds(pl.multiple_of(k * width, width), width)

    sib = device(z, x, y, 1 - c)
    xdev = device(z, 1 - x, y, c)
    ydev = device(z, x, 1 - y, c)
    own_b = mine
    x_b = block(1 - x, y, c)
    y_b = block(x, 1 - y, c)
    d_b = block(1 - x, 1 - y, c)

    def own_copy(k, role, dev):
        return pltpu.make_async_remote_copy(
            src_ref=x_ref.at[:, cols_of(k, WIDTH)],
            dst_ref=xall.at[k, rows_of(own_b)],
            send_sem=x_send.at[k, role], recv_sem=x_recv.at[k, role],
            device_id=dev, device_id_type=MESH,
        )

    def relay_copy(k, role, b, dev):
        return pltpu.make_async_remote_copy(
            src_ref=xall.at[k, rows_of(b)],
            dst_ref=xall.at[k, rows_of(b)],
            send_sem=x_send.at[k, role], recv_sem=x_recv.at[k, role],
            device_id=dev, device_id_type=MESH,
        )

    def x_copies(k):
        return [
            own_copy(k, 0, xdev), own_copy(k, 1, ydev), relay_copy(k, 2, y_b, xdev),
            own_copy(k, 3, sib), relay_copy(k, 4, x_b, sib), relay_copy(k, 5, y_b, sib),
            relay_copy(k, 6, d_b, sib),
        ]

    def start_own(k):
        cs = x_copies(k)
        cs[0].start()
        cs[3].start()

    def relay_far(k):
        cs = x_copies(k)
        cs[1].wait_recv()
        cs[2].start()
        cs[5].start()
        cs[0].wait_recv()
        cs[4].start()

    def relay_near(k):
        cs = x_copies(k)
        cs[2].wait_recv()
        cs[6].start()

    def ct_copy(t, r):
        px, py, pc = peer(r)
        return pltpu.make_async_remote_copy(
            src_ref=ct_ref.at[py * 2 + pc, t * 2 + px],
            dst_ref=ctall.at[t, :, rows_of(mine)],
            send_sem=c_send.at[t, r], recv_sem=c_recv.at[t, r],
            device_id=device(z, px, py, pc), device_id_type=MESH,
        )

    def ct_start(t):
        @pl.loop(1, 8)
        def _(r):
            ct_copy(t, r).start()

    def ct_wait(t):
        @pl.loop(1, 8)
        def _(r):
            ct_copy(t, r).wait_recv()

    half = nz // 2

    def dest(i):
        down = nz - 1 - i
        down = jnp.where(down <= z, down - 1, down)
        up = jnp.where(i >= z, i + 1, i)
        return jnp.where(z < half, down, up)

    def att_copy(a, src, dst, j):
        p = lax.rem(grp + j, members)
        return pltpu.make_async_remote_copy(
            src_ref=src.at[:, cols_of(p, span)],
            dst_ref=dst.at[grp],
            send_sem=a_send.at[a, j], recv_sem=a_recv.at[a, j],
            device_id={"dp": dp, "grp": p}, device_id_type=MESH,
        )

    pairs = ((q_ref, qb), (k_ref, kb), (v_ref, vb), (g_ref, gb))

    def att_start(which):
        for a in which:
            for j in range(1, members):
                att_copy(a, *pairs[a], j).start()

    def back_copy(h, o, j):
        p = lax.rem(grp + j, members)
        return pltpu.make_async_remote_copy(
            src_ref=res.at[h, o, p], dst_ref=back.at[h, o, grp],
            send_sem=b_send.at[h, o, j], recv_sem=b_recv.at[h, o, j],
            device_id={"dp": dp, "grp": p}, device_id_type=MESH,
        )

    def head(h):
        cols = cols_of(h, HEAD_DIM)
        nt = (((1,), (1,)), ((), ()))
        kh = kb[:, :, cols].reshape(members * mem_rows, HEAD_DIM)
        vh = vb[:, :, cols].reshape(members * mem_rows, HEAD_DIM)

        @pl.loop(0, members)
        def _(m):
            qh = qb[m, :, cols]
            gh = gb[m, :, cols]
            s = lax.dot_general(qh, kh, nt, preferred_element_type=F32) * inv_root
            s = jnp.where(mask_ref[m] > 0, s, -1e30)
            w = jnp.exp(s - jnp.max(s, axis=1, keepdims=True))
            p = (w / jnp.sum(w, axis=1, keepdims=True)).astype(BF16)
            o = jnp.dot(p, vh, preferred_element_type=F32).astype(BF16)
            gp = lax.dot_general(gh, vh, nt, preferred_element_type=F32)
            rd = jnp.sum(gh.astype(F32) * o.astype(F32), axis=1, keepdims=True)
            gs = (p.astype(F32) * (gp - rd)).astype(BF16)
            res[h, 0, m] = o
            res[h, 1, m] = (jnp.dot(gs, kh, preferred_element_type=F32) * inv_root).astype(BF16)

        for o in range(2):
            for j in range(1, members):
                back_copy(h, o, j).start()

    def z_copy(t, k):
        right = t > z
        nxt = jnp.where(right, z + 1, z - 1)
        nxt = jnp.minimum(jnp.maximum(nxt, 0), nz - 1)
        slot = jnp.where(jnp.logical_and(nxt == t, t < z), nz, t)
        return pltpu.make_async_remote_copy(
            src_ref=outgo.at[t, k], dst_ref=income.at[slot, k],
            send_sem=z_send.at[t, k], recv_sem=z_recv.at[slot, k],
            device_id=device(nxt, x, y, c), device_id_type=MESH,
        )

    def z_wait(slot, k):
        pltpu.make_async_remote_copy(
            src_ref=income.at[slot, k], dst_ref=income.at[slot, k],
            send_sem=z_send.at[0, k], recv_sem=z_recv.at[slot, k],
            device_id=sib, device_id_type=MESH,
        ).wait_recv()

    def part(t, k):
        return jnp.dot(ctall[t], xall[k], preferred_element_type=F32)

    def push(k):
        @pl.loop(0, nz - 1)
        def _(i):
            t = dest(i)

            @pl.when(k == 0)
            def _():
                ct_wait(t)

            value = part(t, k)
            has = jnp.where(t > z, z > 0, z < nz - 1)

            @pl.when(has)
            def _():
                z_wait(t, k)
                outgo[t, k] = (value + income[t, k].astype(F32)).astype(BF16)

            @pl.when(jnp.logical_not(has))
            def _():
                outgo[t, k] = value.astype(BF16)

            z_copy(t, k).start()

    def finish(k):
        cols = cols_of(k, WIDTH)
        up_ref[:, cols] = part(z, k)

        @pl.when(z > 0)
        def _():
            z_wait(z, k)
            up_ref[:, cols] += income[z, k].astype(F32)

        @pl.when(z < nz - 1)
        def _():
            z_wait(nz, k)
            up_ref[:, cols] += income[nz, k].astype(F32)

    for t in range(nz):
        ctall[t, :, rows_of(mine)] = ct_ref[grp, t * 2 + x]
    local = [
        pltpu.make_async_copy(
            x_ref.at[:, pl.ds(k * WIDTH, WIDTH)], xall.at[k, rows_of(mine)], l_sem.at[k]
        )
        for k in range(chunks)
    ] + [
        pltpu.make_async_copy(src.at[:, cols_of(grp, span)], dst.at[grp], l_sem.at[chunks + a])
        for a, (src, dst) in enumerate(pairs)
    ]
    for copy in local:
        copy.start()

    others = 7 + jnp.where(z > 0, 1, 0) + jnp.where(z < nz - 1, 1, 0)
    pl.semaphore_wait(barrier, others)

    ct_start(dest(0))
    start_own(0)
    for k in range(2):
        x_copies(k)[1].start()
    ct_start(dest(1))
    relay_far(0)
    start_own(1)

    @pl.loop(2, nz - 1)
    def _(i):
        ct_start(dest(i))

    relay_near(0)
    relay_far(1)
    start_own(2)
    for k in range(2, chunks):
        x_copies(k)[1].start()

    first_head = chunks // 2
    per_step = pl.cdiv(heads, chunks - first_head)
    lag = min(3, chunks - 2)

    for copy in local:
        copy.wait()

    @pl.loop(0, chunks)
    def _(k):
        for role in range(3, 7):
            x_copies(k)[role].wait_recv()
        push(k)

        @pl.when(k + 1 < chunks)
        def _():
            relay_near(k + 1)

        @pl.when(k + 2 < chunks)
        def _():
            relay_far(k + 2)

        @pl.when(k + 3 < chunks)
        def _():
            start_own(k + 3)

        @pl.when(k == 0)
        def _():
            ct_start(z)
            pass

        @pl.when(k == 1)
        def _():
            att_start((0, 1))

        @pl.when(k == 2)
        def _():
            att_start((2, 3))

        @pl.when(k == first_head)
        def _():
            for a in range(4):
                for j in range(1, members):
                    att_copy(a, *pairs[a], j).wait_recv()

        for n in range(per_step):
            h = (k - first_head) * per_step + n

            @pl.when(jnp.logical_and(k >= first_head, h < heads))
            def _(h=h):
                head(h)

        @pl.when(k == lag)
        def _():
            ct_wait(z)

        @pl.when(k >= lag)
        def _():
            finish(k - lag)

    @pl.loop(chunks - lag, chunks)
    def _(k):
        finish(k)

    for o, ref in ((0, attn_ref), (1, qgrad_ref)):
        for h in range(heads):
            for j in range(1, members):
                back_copy(h, o, j).wait_recv()
                p = lax.rem(grp + members - j, members)
                ref[:, pl.ds(pl.multiple_of(p * span + h * HEAD_DIM, HEAD_DIM), HEAD_DIM)] = back[h, o, p]
            ref[:, pl.ds(pl.multiple_of(grp * span + h * HEAD_DIM, HEAD_DIM), HEAD_DIM)] = res[h, o, grp]

    @pl.loop(0, chunks)
    def _(k):
        for copy in x_copies(k):
            copy.wait_send()

        @pl.loop(0, nz - 1)
        def _(i):
            z_copy(dest(i), k).wait_send()

    @pl.loop(0, nz)
    def _(t):
        @pl.loop(1, 8)
        def _(r):
            ct_copy(t, r).wait_send()

    for a in range(4):
        for j in range(1, members):
            att_copy(a, *pairs[a], j).wait_send()

    @pl.loop(0, heads)
    def _(h):
        for o in range(2):
            for j in range(1, members):
                back_copy(h, o, j).wait_send()


def fused_call(
    nz, queries, mem_keys, mem_values, lengths, mates, out_grad, mlp_input, gate_pre, hidden_grad
):
    members = lax.axis_size("grp")
    groups = lax.axis_size("dp")
    rows, width = queries.shape[2:]
    mem_rows = mem_keys.shape[2]
    model, hidden = mlp_input.shape[3], gate_pre.shape[3]
    span = width // members
    heads = span // HEAD_DIM
    own = hidden // (members * groups)
    layer = 2 * members
    chunks = model // WIDTH
    up_cot = (
        hidden_grad[0, 0].astype(F32) * jax.nn.silu(gate_pre[0, 0].astype(F32))
    ).astype(BF16)
    ct = up_cot.T.reshape(members, groups, own, rows)
    allowed = (mates[0] > 0) | jnp.eye(members, dtype=bool)
    live = jnp.arange(mem_rows, dtype=jnp.int32)[None, :] < lengths[0][:, None]
    mask = (allowed[:, :, None] & live[None]).astype(F32).reshape(members, 1, members * mem_rows)
    vm = pl.BlockSpec(memory_space=pltpu.VMEM)
    dma = pltpu.SemaphoreType.DMA
    attn, qgrad, up = pl.pallas_call(
        functools.partial(fused_kernel, nz),
        out_shape=(
            jax.ShapeDtypeStruct((rows, width), BF16),
            jax.ShapeDtypeStruct((rows, width), BF16),
            jax.ShapeDtypeStruct((own, model), F32),
        ),
        in_specs=[vm] + [pl.BlockSpec(memory_space=pltpu.HBM)] * 5 + [vm],
        out_specs=(vm, vm, vm),
        scratch_shapes=[
            pltpu.VMEM((chunks, layer * rows, WIDTH), BF16),
            pltpu.VMEM((nz, own, layer * rows), BF16),
            pltpu.VMEM((members, rows, span), BF16),
            pltpu.VMEM((members, mem_rows, span), BF16),
            pltpu.VMEM((members, mem_rows, span), BF16),
            pltpu.VMEM((members, rows, span), BF16),
            pltpu.VMEM((heads, 2, members, rows, HEAD_DIM), BF16),
            pltpu.VMEM((heads, 2, members, rows, HEAD_DIM), BF16),
            pltpu.VMEM((nz, chunks, own, WIDTH), BF16),
            pltpu.VMEM((nz + 1, chunks, own, WIDTH), BF16),
            dma((chunks, 7)), dma((chunks, 7)),
            dma((nz, 8)), dma((nz, 8)),
            dma((4, members)), dma((4, members)),
            dma((heads, 2, members)), dma((heads, 2, members)),
            dma((nz, chunks)), dma((nz + 1, chunks)), dma((chunks + 4,)),
        ],
        compiler_params=pltpu.CompilerParams(
            collective_id=0, has_side_effects=True, vmem_limit_bytes=44 * 1024 * 1024
        ),
        name="fused",
    )(
        mask, queries[0, 0], mem_keys[0, 0], mem_values[0, 0], out_grad[0, 0], mlp_input[0, 0], ct
    )
    return attn[None, None], qgrad[None, None], up.T


def choose(*args):
    members, groups = lax.axis_size("grp"), lax.axis_size("dp")
    near = 1 << ((groups.bit_length() - 1) // 2)
    hidden, model = args[7].shape[3], args[6].shape[3]
    own = hidden // (members * groups)
    fits = members == 4 and near == 2 and groups % 2 == 0 and own % 16 == 0 and model % WIDTH == 0
    if fits and model // WIDTH >= 4:
        return fused_call(groups // near, *args)
    return per_device(*args)


def solution(mesh):
    return jax.shard_map(
        choose,
        mesh=mesh,
        in_specs=(
            P("dp", "grp", None, None),
            P("dp", "grp", None, None),
            P("dp", "grp", None, None),
            P("dp", None),
            P("dp", None, None),
            P("dp", "grp", None, None),
            P("dp", "grp", None, None),
            P("dp", "grp", None, None),
            P("dp", "grp", None, None),
        ),
        out_specs=(P("dp", "grp", None, None), P("dp", "grp", None, None), P(None, ("grp", "dp"))),
        check_vma=False,
    )
```
